32 devices in a mesh: clips: 2 (over y), tm: 4 (over x, core), rows: 4 (over z).
Axes of the slice: x: 2, y: 2, z: 4, core: 2. Of those that a mesh axis runs over, the one named last changes fastest.
Arguments:
- features: bfloat16 [64, 16, 32, 192], P(('clips', 'tm'), 'rows'), parts along dimension 0, may hold values from -6 to 6
- norm_gain: float32 [192], replicated, may hold values from 0.1 to 1.9
- conv_weight: bfloat16 [3, 3, 3, 192, 96], replicated, may hold values from -0.078125 to 0.078125
- out_grad: bfloat16 [64, 16, 32, 96], P(('clips', 'tm'), 'rows'), parts along dimension 0, may hold values from -6 to 6
Outputs:
- grad_features: bfloat16 [64, 16, 32, 192], P(('clips', 'tm'), 'rows'), parts along dimension 0
- grad_weight: float32 [6, 3, 3, 192, 96], P('clips'), parts along dimension 0
The draws below stay inside these ranges and needn't reach their ends.
There are 2 independent parts, one for each index of `clips`. The reference program is written for one: setup_inputs(seed, part) draws one part's arguments, and reference() takes and returns one part's arrays. A program takes and returns all parts, laid end to end along the dimension named above; an argument that names none is the same for every part. Nothing has to cross between parts.
All inputs are finite; a program needn't handle non-finite values.
Results may differ from the reference program's by a relative error of at most 0.0029.
Values may be sent and summed in bfloat16 or wider, within the bound.
A program may use at most 64 MiB of HBM per device.

```python
import jax
import jax.numpy as jnp
from jax import lax

CIN = 192
COUT = 96
WIDTH = 32
FRAMES = 32
ROWS = 16
POSITIONS = 16384


def block_scale(stream_key, extent, split, least, high):
    factor_of, own = 1.0, jax.random.fold_in(stream_key, 6)
    for position, parts in split:
        draws = jnp.exp(jax.random.uniform(jax.random.fold_in(own, position), (parts,), jnp.float32, least / len(split), high / len(split)))
        factor_of = factor_of * jnp.repeat(draws, extent[position] // parts).reshape([-1 if axis == position else 1 for axis in range(len(extent))])
    return factor_of


def normal_values(stream_key, dims, scale, most, shards=(), dtype=jnp.bfloat16):
    values = scale * jax.random.normal(stream_key, dims, jnp.float32)
    if shards:
        values = values * block_scale(stream_key, dims, shards, -0.22, 0.18)
    return jnp.clip(values, -most, most).astype(dtype)


def setup_inputs(seed: int = 0, part: int = 0) -> dict:
    seeds = jax.random.split(jax.random.key(seed), 5)
    own_keys = jax.random.split(jax.random.fold_in(seeds[4], part), 5)
    features = normal_values(own_keys[0], (FRAMES, ROWS, WIDTH, CIN), 1.0, 6.0, ((0, 4), (1, 4)))
    norm_gain = jnp.clip(1.0 + 0.18 * jax.random.normal(seeds[1], (CIN,), jnp.float32), 0.1, 1.9)
    conv_weight = normal_values(seeds[2], (3, 3, 3, CIN, COUT), (27 * CIN) ** -0.5, 0.078125)
    out_grad = normal_values(own_keys[3], (FRAMES, ROWS, WIDTH, COUT), 1.0, 6.0, ((0, 4), (1, 4)))
    return dict(features=features, norm_gain=norm_gain, conv_weight=conv_weight, out_grad=out_grad)


def activate(features, norm_gain):
    values = features.astype(jnp.float32)
    inv_rms = lax.rsqrt(lax.optimization_barrier(jnp.mean(values * values, axis=-1, keepdims=True)) + 1e-06)
    unit = values * inv_rms
    normed = unit * norm_gain
    return (normed, inv_rms, unit)

def reference(features, norm_gain, conv_weight, out_grad):
    normed, inv_rms, unit = activate(features, norm_gain)
    act = jax.nn.silu(normed).astype(jnp.bfloat16)
    frames, height, width = (act.shape[0], act.shape[1], act.shape[2])
    act_pad = jnp.pad(act, ((2, 0), (1, 1), (1, 1), (0, 0)))
    out_pad = jnp.pad(out_grad, ((0, 2), (1, 1), (1, 1), (0, 0)))
    count = frames * height * width
    grad_act = jnp.zeros((count, CIN), jnp.float32)
    kernel_terms = []
    flat_out = out_grad.reshape(count, COUT)
    for i in range(3):
        for j in range(3):
            for k in range(3):
                shifted = out_pad[2 - i:2 - i + frames, 2 - j:2 - j + height, 2 - k:2 - k + width].reshape(count, COUT)
                grad_act = grad_act + jnp.dot(shifted, conv_weight[i, j, k].T, preferred_element_type=jnp.float32)
                window = act_pad[i:i + frames, j:j + height, k:k + width].reshape(count, CIN)
                kernel_terms.append(jnp.dot(window.T, flat_out, preferred_element_type=jnp.float32))
    grad_weight = jnp.stack(kernel_terms).reshape(3, 3, 3, CIN, COUT) * (1.0 / jnp.sqrt(jnp.float32(POSITIONS)))
    grad_act = grad_act.reshape(frames, height, width, CIN)
    sigma = jax.nn.sigmoid(normed)
    grad_normed = grad_act * sigma * (1.0 + normed * (1.0 - sigma))
    grad_unit = grad_normed * norm_gain
    grad_features = inv_rms * (grad_unit - unit * lax.optimization_barrier(jnp.mean(grad_unit * unit, axis=-1, keepdims=True)))
    return (grad_features.astype(jnp.bfloat16), grad_weight)
```

```python
import functools
import math

import jax
import jax.numpy as jnp
from jax import lax
from jax.experimental import pallas as pl
from jax.experimental.pallas import tpu as pltpu
from jax.sharding import PartitionSpec as P

LANES = 128
SUB = 16
MESH = pl.DeviceIdType.MESH
NT = (((1,), (1,)), ((), ()))


def shift_lanes(x, shift):
    shift = shift % LANES
    return x if shift == 0 else pltpu.roll(x, shift, 1)


def rearrange(sources, source_width, target_start, target_width):
    lane = lax.broadcasted_iota(jnp.int32, (1, LANES), 1)
    value = None
    for a, source in enumerate(sources):
        first = a * source_width - target_start
        if first >= target_width or first + source_width <= 0:
            continue
        moved = shift_lanes(source, first)
        value = moved if value is None else jnp.where(lane >= first, moved, value)
    return value


def kernel(
    dims,
    features, gain, weight, grad,
    gf_ref, out_ref,
    padded, shifted, wide, act_t, acc, parts, gwf, send_a, recv_a, sum_a,
    send_b, recv_b, sum_b, send_c, recv_c, gath,
    halo_s, halo_r, sa, ra, sb, rb, sc, rc, sc2, rc2, sb2, rb2, sa2, ra2, out_sem,
):
    T, R, PR, X, m = dims
    frames, height, width, channels = features.shape
    outputs = grad.shape[3]
    taps = weight.shape[0]
    tm, z = lax.axis_index("tm"), lax.axis_index("rows")
    pair, x = lax.rem(tm, PR), lax.div(tm, PR)

    barrier = pltpu.get_barrier_semaphore()
    for d in range(1, T * R):
        peer = lax.rem(tm * R + z + d, T * R)
        pl.semaphore_signal(
            barrier, inc=1, device_id={"tm": lax.div(peer, R), "rows": lax.rem(peer, R)},
            device_id_type=MESH,
        )

    up, down, later, earlier = z > 0, z < R - 1, tm < T - 1, tm > 0
    own = pl.ds(1, height)
    tail = pl.ds(frames, 2)
    body = pl.ds(0, frames)
    halos = (
        (down, (tm, z + 1), up, grad.at[:, height - 1], padded.at[body, 0]),
        (up, (tm, z - 1), down, grad.at[:, 0], padded.at[body, height + 1]),
        (earlier, (tm - 1, z), later, grad.at[pl.ds(0, 2)], padded.at[tail, own]),
        (jnp.logical_and(earlier, down), (tm - 1, z + 1), jnp.logical_and(later, up),
         grad.at[pl.ds(0, 2), height - 1], padded.at[tail, 0]),
        (jnp.logical_and(earlier, up), (tm - 1, z - 1), jnp.logical_and(later, down),
         grad.at[pl.ds(0, 2), 0], padded.at[tail, height + 1]),
    )

    def halo(n):
        _, to, _, source, target = halos[n]
        return pltpu.make_async_remote_copy(
            src_ref=source, dst_ref=target, send_sem=halo_s.at[n], recv_sem=halo_r.at[n],
            device_id={"tm": to[0], "rows": to[1]}, device_id_type=MESH,
        )

    for n, (_, _, receives, _, target) in enumerate(halos):
        @pl.when(jnp.logical_not(receives))
        def _():
            target[...] = jnp.zeros(target.shape, target.dtype)

    pl.semaphore_wait(barrier, T * R - 1)
    for n in range(5):
        @pl.when(halos[n][0])
        def _():
            halo(n).start()

    def activate(f):
        values = features[f].reshape(height * width, channels).astype(jnp.float32)
        inv_rms = lax.rsqrt(jnp.sum(values * values, axis=-1, keepdims=True) / channels + 1e-06)
        unit = values * inv_rms
        normed = unit * gain[...]
        sigma = 1.0 / (1.0 + jnp.exp(-normed))
        return inv_rms, unit, normed, sigma

    for f in range(frames):
        _, _, normed, sigma = activate(f)
        act = (normed * sigma).astype(jnp.bfloat16)
        act_t[:, f * height * width:(f + 1) * height * width] = act.T
        padded[f, 1:1 + height] = grad[f]

    wide[...] = jnp.zeros(wide.shape, wide.dtype)
    for t in range(taps):
        wide[:, t * LANES:t * LANES + outputs] = weight[t]
    shifted[...] = jnp.zeros(shifted.shape, shifted.dtype)

    for n in range(5):
        @pl.when(halos[n][2])
        def _():
            halo(n).wait_recv()

    rows = (height + 2) * width
    column = lax.rem(lax.broadcasted_iota(jnp.int32, (rows, LANES), 0), width)
    for f in range(frames + 2):
        shifted[f, :, :, LANES:LANES + outputs] = padded[f]
        middle = shifted[f, :, :, LANES:2 * LANES].reshape(rows, LANES).astype(jnp.float32)
        after = jnp.where(column == width - 1, 0.0, pltpu.roll(middle, rows - 1, 0))
        before = jnp.where(column == 0, 0.0, pltpu.roll(middle, 1, 0))
        shape = (height + 2, width, LANES)
        shifted[f, :, :, 0:LANES] = after.astype(jnp.bfloat16).reshape(shape)
        shifted[f, :, :, 2 * LANES:3 * LANES] = before.astype(jnp.bfloat16).reshape(shape)

    count = frames * height * width

    def window(i):
        return jnp.concatenate(
            [
                shifted[2 - i:2 - i + frames, 2 - j:2 - j + height].reshape(count, 3 * LANES)
                for j in range(3)
            ],
            axis=1,
        )

    for i in range(3):
        terms = jnp.dot(act_t[...], window(i), preferred_element_type=jnp.float32)
        for t in range(9):
            parts[9 * i + t] = terms[:, t * LANES:(t + 1) * LANES]

    group = LANES // math.gcd(LANES, outputs)
    per_group = group * outputs // LANES
    row_tiles = channels // SUB
    total = T * R * m
    stored = 0

    def place(n):
        n, s = divmod(n, m)
        n, xx = divmod(n, X)
        pp, c = divmod(n, R)
        return pp, c, xx, s

    for g in range(-(-taps // group)):
        sources = [parts[t] for t in range(g * group, min(taps, (g + 1) * group))]
        for lt in range(per_group):
            tile = rearrange(sources, outputs, lt * LANES, LANES)
            for rt in range(row_tiles):
                where = place(stored)
                piece = tile[rt * SUB:(rt + 1) * SUB]
                gwf[where] = piece
                send_a[where] = piece.astype(jnp.bfloat16)
                stored += 1
    while stored < total:
        gwf[place(stored)] = jnp.zeros((SUB, LANES), jnp.float32)
        send_a[place(stored)] = jnp.zeros((SUB, LANES), jnp.bfloat16)
        stored += 1

    def remote(source, target, send, recv, to_tm, to_z):
        return pltpu.make_async_remote_copy(
            src_ref=source, dst_ref=target, send_sem=send, recv_sem=recv,
            device_id={"tm": to_tm, "rows": to_z}, device_id_type=MESH,
        )

    mate = x * PR + (1 - pair if PR == 2 else pair)

    def chunk(d):
        return lax.rem(z + d, R)

    def stage_a(d):
        c = chunk(d)
        return remote(send_a.at[1 - pair, c], recv_a.at[d - 1], sa.at[d - 1], ra.at[d - 1], mate, z)

    def side(e):
        return lax.rem(x + e, X)

    def stage_b(d, e):
        return remote(
            send_b.at[d - 1, side(e)], recv_b.at[d - 1, e - 1],
            sb.at[d - 1, e - 1], rb.at[d - 1, e - 1], side(e) * PR + pair, z,
        )

    def stage_c(d):
        return remote(send_c.at[d - 1], recv_c.at[d - 1], sc.at[d - 1], rc.at[d - 1], tm, chunk(d))

    def gather_c(d):
        piece = gath.at[pair, z, x]
        return remote(piece, piece, sc2.at[d - 1], rc2.at[d - 1], tm, chunk(d))

    def gather_b(d, e):
        piece = gath.at[pair, lax.rem(z + R - d + R, R), x]
        return remote(piece, piece, sb2.at[d - 1, e - 1], rb2.at[d - 1, e - 1], side(e) * PR + pair, z)

    def gather_a(d):
        piece = gath.at[pair, lax.rem(z + R - d + R, R)]
        return remote(piece, piece, sa2.at[d - 1], ra2.at[d - 1], mate, z)

    order = range(1, R + 1)
    if PR == 2:
        for d in order:
            stage_a(d).start()

    def conv(i):
        weights = wide[:, 9 * LANES * i:9 * LANES * (i + 1)]
        return lax.dot_general(window(i), weights, NT, preferred_element_type=jnp.float32)

    acc[...] = conv(0)

    for d in order:
        value = gwf[pair, chunk(d)]
        if PR == 2:
            stage_a(d).wait_recv()
            value = value + recv_a[d - 1].astype(jnp.float32)
        sum_a[d - 1] = value
        send_b[d - 1] = value.astype(jnp.bfloat16)
        for e in range(1, X):
            stage_b(d, e).start()

    acc[...] += conv(1)

    for d in order:
        value = sum_a[d - 1, x]
        for e in range(1, X):
            stage_b(d, e).wait_recv()
            value = value + recv_b[d - 1, e - 1].astype(jnp.float32)
        if d < R:
            send_c[d - 1] = value.astype(jnp.bfloat16)
            stage_c(d).start()
        else:
            sum_b[...] = value

    acc[...] += conv(2)

    value = sum_b[...]
    for d in range(1, R):
        stage_c(d).wait_recv()
        value = value + recv_c[d - 1].astype(jnp.float32)
    gath[pair, z, x] = value.astype(jnp.bfloat16)
    for d in range(1, R):
        gather_c(d).start()
    for e in range(1, X):
        gather_b(R, e).start()

    for f in range(frames):
        inv_rms, unit, normed, sigma = activate(f)
        grad_act = acc[f * height * width:(f + 1) * height * width]
        grad_normed = grad_act * sigma * (1.0 + normed * (1.0 - sigma))
        grad_unit = grad_normed * gain[...]
        along = jnp.sum(grad_unit * unit, axis=-1, keepdims=True) / channels
        result = inv_rms * (grad_unit - unit * along)
        gf_ref[f] = result.astype(jnp.bfloat16).reshape(height, width, channels)

    for d in range(1, R):
        gather_c(d).wait_recv()
        for e in range(1, X):
            gather_b(d, e).start()
    for d in (R, *range(1, R)):
        for e in range(1, X):
            gather_b(d, e).wait_recv()
        if PR == 2:
            gather_a(d).start()
    for d in (R, *range(1, R)):
        if PR == 2:
            gather_a(d).wait_recv()

    result_copy = pltpu.make_async_copy(gath, out_ref, out_sem)
    result_copy.start()
    for n in range(5):
        @pl.when(halos[n][0])
        def _():
            halo(n).wait_send()
    for d in order:
        if PR == 2:
            stage_a(d).wait_send()
            gather_a(d).wait_send()
        for e in range(1, X):
            stage_b(d, e).wait_send()
            gather_b(d, e).wait_send()
        if d < R:
            stage_c(d).wait_send()
            gather_c(d).wait_send()
    result_copy.wait()


def unpack(outputs, row_tiles, scale, tiles, out):
    group, per_group = out.shape[0], tiles.shape[0] // row_tiles
    sources = [
        tiles[lt * row_tiles:(lt + 1) * row_tiles].astype(jnp.float32).reshape(row_tiles * SUB, LANES)
        for lt in range(per_group)
    ]
    for a in range(group):
        value = rearrange(sources, LANES, a * outputs, outputs)
        out[a] = value[:, :outputs] * scale


def on_device(features, norm_gain, conv_weight, out_grad):
    frames, height, width, channels = features.shape
    outputs = out_grad.shape[3]
    T, R = lax.axis_size("tm"), lax.axis_size("rows")
    PR = 2 if T % 2 == 0 else 1
    X = T // PR
    kernels = conv_weight.shape[:3]
    taps = math.prod(kernels)
    group = LANES // math.gcd(LANES, outputs)
    per_group = group * outputs // LANES
    row_tiles = channels // SUB
    groups = -(-taps // group)
    m = -(-(groups * per_group * row_tiles) // (T * R))
    count = frames * height * width
    bf16, f32 = jnp.bfloat16, jnp.float32
    vmem, dma = pltpu.VMEM, pltpu.SemaphoreType.DMA
    tile = (m, SUB, LANES)
    rest = max(R - 1, 1)
    sides = max(X - 1, 1)
    in_vmem = pl.BlockSpec(memory_space=pltpu.VMEM)
    grad_features, gathered = pl.pallas_call(
        functools.partial(kernel, (T, R, PR, X, m)),
        out_shape=(
            jax.ShapeDtypeStruct(features.shape, bf16),
            jax.ShapeDtypeStruct((PR, R, X) + tile, bf16),
        ),
        in_specs=[in_vmem] * 4,
        out_specs=(in_vmem, pl.BlockSpec(memory_space=pl.ANY)),
        scratch_shapes=[
            vmem((frames + 2, height + 2, width, outputs), bf16),
            vmem((frames + 2, height + 2, width, 3 * LANES), bf16),
            vmem((channels, taps * LANES), bf16),
            vmem((channels, count), bf16),
            vmem((count, channels), f32),
            vmem((taps, channels, LANES), f32),
            vmem((PR, R, X) + tile, f32),
            vmem((PR, R, X) + tile, bf16),
            vmem((R, X) + tile, bf16),
            vmem((R, X) + tile, f32),
            vmem((R, X) + tile, bf16),
            vmem((R, sides) + tile, bf16),
            vmem(tile, f32),
            vmem((rest,) + tile, bf16),
            vmem((rest,) + tile, bf16),
            vmem((PR, R, X) + tile, bf16),
            dma((5,)), dma((5,)),
            dma((R,)), dma((R,)),
            dma((R, sides)), dma((R, sides)),
            dma((rest,)), dma((rest,)),
            dma((rest,)), dma((rest,)),
            dma((R, sides)), dma((R, sides)),
            dma((R,)), dma((R,)),
            dma(()),
        ],
        compiler_params=pltpu.CompilerParams(
            collective_id=0, has_side_effects=True, vmem_limit_bytes=50 * 1024 * 1024
        ),
    )(
        features, norm_gain.reshape(1, channels),
        conv_weight.reshape(taps, channels, outputs), out_grad,
    )
    scale = 1.0 / math.sqrt(count * T * R)
    grad_weight = pl.pallas_call(
        functools.partial(unpack, outputs, row_tiles, scale),
        grid=(groups,),
        in_specs=[pl.BlockSpec((per_group * row_tiles, SUB, LANES), lambda g: (g, 0, 0))],
        out_specs=pl.BlockSpec((group, channels, outputs), lambda g: (g, 0, 0)),
        out_shape=jax.ShapeDtypeStruct((taps, channels, outputs), f32),
    )(gathered.reshape(T * R * m, SUB, LANES))
    return grad_features, grad_weight.reshape(kernels + (channels, outputs))


def solution(mesh):
    split = P(("clips", "tm"), "rows", None, None)
    return jax.shard_map(
        on_device,
        mesh=mesh,
        in_specs=(split, P(), P(), split),
        out_specs=(split, P("clips", None, None, None, None)),
        check_vma=False,
    )
```

```python
import functools
import math

import jax
import jax.numpy as jnp
from jax import lax
from jax.experimental import pallas as pl
from jax.experimental.pallas import tpu as pltpu
from jax.sharding import PartitionSpec as P

LANES = 128
SUB = 16
MESH = pl.DeviceIdType.MESH
NT = (((1,), (1,)), ((), ()))


def shift_lanes(x, shift):
    shift = shift % LANES
    return x if shift == 0 else pltpu.roll(x, shift, 1)


def rearrange(sources, source_width, target_start, target_width):
    lane = lax.broadcasted_iota(jnp.int32, (1, LANES), 1)
    value = None
    for a, source in enumerate(sources):
        first = a * source_width - target_start
        if first >= target_width or first + source_width <= 0:
            continue
        moved = shift_lanes(source, first)
        value = moved if value is None else jnp.where(lane >= first, moved, value)
    return value


def kernel(
    dims,
    features_hbm, gain_hbm, weight_hbm, grad,
    gf_ref, out_ref,
    features, gain, weight, padded, shifted, wide, act_t, acc, parts, gwf, recv_a, sum_a,
    send_b, recv_b, sum_b, send_c, recv_c, gath,
    local, halo_s, halo_r, sa, ra, sb, rb, sc, rc, sc2, rc2, sb2, rb2, sa2, ra2,
):
    T, R, PR, X, U, m = dims
    frames, height, width, channels = features.shape
    outputs = grad.shape[3]
    taps = weight.shape[0]
    tm, z = lax.axis_index("tm"), lax.axis_index("rows")
    pair, x = lax.rem(tm, PR), lax.div(tm, PR)
    own = pl.ds(1, height)
    tail = pl.ds(frames, 2)
    body = pl.ds(0, frames)

    loads = [
        pltpu.make_async_copy(source, target, local.at[n])
        for n, (source, target) in enumerate((
            (features_hbm, features), (gain_hbm, gain),
            (grad, padded.at[body, own]), (weight_hbm, weight),
        ))
    ]
    for load in loads:
        load.start()

    barrier = pltpu.get_barrier_semaphore()
    for d in range(1, T * R):
        peer = lax.rem(tm * R + z + d, T * R)
        pl.semaphore_signal(
            barrier, inc=1, device_id={"tm": lax.div(peer, R), "rows": lax.rem(peer, R)},
            device_id_type=MESH,
        )

    up, down, later, earlier = z > 0, z < R - 1, tm < T - 1, tm > 0
    halos = (
        (down, (tm, z + 1), up, grad.at[:, height - 1], padded.at[body, 0]),
        (up, (tm, z - 1), down, grad.at[:, 0], padded.at[body, height + 1]),
        (earlier, (tm - 1, z), later, grad.at[pl.ds(0, 2)], padded.at[tail, own]),
        (jnp.logical_and(earlier, down), (tm - 1, z + 1), jnp.logical_and(later, up),
         grad.at[pl.ds(0, 2), height - 1], padded.at[tail, 0]),
        (jnp.logical_and(earlier, up), (tm - 1, z - 1), jnp.logical_and(later, down),
         grad.at[pl.ds(0, 2), 0], padded.at[tail, height + 1]),
    )

    def halo(n):
        _, to, _, source, target = halos[n]
        return pltpu.make_async_remote_copy(
            src_ref=source, dst_ref=target, send_sem=halo_s.at[n], recv_sem=halo_r.at[n],
            device_id={"tm": to[0], "rows": to[1]}, device_id_type=MESH,
        )

    for n, (_, _, receives, _, target) in enumerate(halos):
        @pl.when(jnp.logical_not(receives))
        def _():
            target[...] = jnp.zeros(target.shape, target.dtype)
    shifted[:, :, :, LANES:2 * LANES] = jnp.zeros(shifted.shape[:3] + (LANES,), shifted.dtype)

    pl.semaphore_wait(barrier, T * R - 1)
    for n in range(5):
        @pl.when(halos[n][0])
        def _():
            halo(n).start()

    def activate(f):
        values = features[f].reshape(height * width, channels).astype(jnp.float32)
        inv_rms = lax.rsqrt(jnp.sum(values * values, axis=-1, keepdims=True) / channels + 1e-06)
        unit = values * inv_rms
        normed = unit * gain[...]
        sigma = 1.0 / (1.0 + jnp.exp(-normed))
        return inv_rms, unit, normed, sigma

    loads[0].wait()
    loads[1].wait()
    for f in range(frames):
        _, _, normed, sigma = activate(f)
        act = (normed * sigma).astype(jnp.bfloat16)
        act_t[:, f * height * width:(f + 1) * height * width] = act.T

    loads[2].wait()
    for n in range(5):
        @pl.when(halos[n][2])
        def _():
            halo(n).wait_recv()

    rows = (height + 2) * width
    column = lax.rem(lax.broadcasted_iota(jnp.int32, (rows, LANES), 0), width)
    for f in range(frames + 2):
        shifted[f, :, :, LANES:LANES + outputs] = padded[f]
        middle = shifted[f, :, :, LANES:2 * LANES].reshape(rows, LANES).astype(jnp.float32)
        after = jnp.where(column == width - 1, 0.0, pltpu.roll(middle, rows - 1, 0))
        before = jnp.where(column == 0, 0.0, pltpu.roll(middle, 1, 0))
        shape = (height + 2, width, LANES)
        shifted[f, :, :, 0:LANES] = after.astype(jnp.bfloat16).reshape(shape)
        shifted[f, :, :, 2 * LANES:3 * LANES] = before.astype(jnp.bfloat16).reshape(shape)

    count = frames * height * width

    def window(i):
        return jnp.concatenate(
            [
                shifted[2 - i:2 - i + frames, 2 - j:2 - j + height].reshape(count, 3 * LANES)
                for j in range(3)
            ],
            axis=1,
        )

    def remote(source, target, send, recv, to_tm, to_z):
        return pltpu.make_async_remote_copy(
            src_ref=source, dst_ref=target, send_sem=send, recv_sem=recv,
            device_id={"tm": to_tm, "rows": to_z}, device_id_type=MESH,
        )

    mate = x * PR + (1 - pair if PR == 2 else pair)

    def chunk(d):
        return lax.rem(z + d, R)

    def back(d):
        return lax.rem(z + 2 * R - d, R)

    def side(e):
        return lax.rem(x + e, X)

    def stage_a(u, d):
        return remote(
            gwf.at[u, 1 - pair, chunk(d)], recv_a.at[u, d - 1],
            sa.at[u, d - 1], ra.at[u, d - 1], mate, z,
        )

    def stage_b(u, d, e):
        return remote(
            send_b.at[u, d - 1, side(e)], recv_b.at[u, d - 1, e - 1],
            sb.at[u, d - 1, e - 1], rb.at[u, d - 1, e - 1], side(e) * PR + pair, z,
        )

    def stage_c(u, d):
        return remote(
            send_c.at[u, d - 1], recv_c.at[u, d - 1],
            sc.at[u, d - 1], rc.at[u, d - 1], tm, chunk(d),
        )

    def gather_c(u, d):
        piece = gath.at[u, pair, z, x]
        return remote(piece, piece, sc2.at[u, d - 1], rc2.at[u, d - 1], tm, chunk(d))

    def gather_b(u, d, e):
        piece = gath.at[u, pair, back(d), x]
        return remote(
            piece, piece, sb2.at[u, d - 1, e - 1], rb2.at[u, d - 1, e - 1],
            side(e) * PR + pair, z,
        )

    def gather_a(u, d):
        piece = gath.at[u, pair, back(d)]
        return remote(piece, piece, sa2.at[u, d - 1], ra2.at[u, d - 1], mate, z)

    order = range(1, R + 1)
    mine_first = (R, *range(1, R))
    group = LANES // math.gcd(LANES, outputs)
    groups = -(-taps // group)
    per_group = group * outputs // LANES
    row_tiles = channels // SUB
    unit_tiles = T * R * m

    def place(n):
        n, s = divmod(n, m)
        n, xx = divmod(n, X)
        n, c = divmod(n, R)
        u, pp = divmod(n, PR)
        return u, pp, c, xx, s

    state = {"stored": 0, "sent": 0}

    def send_ready():
        while (state["sent"] + 1) * unit_tiles <= state["stored"]:
            if PR == 2:
                for d in order:
                    stage_a(state["sent"], d).start()
            state["sent"] += 1

    done = 0
    for i in range(3):
        terms = jnp.dot(act_t[...], window(i), preferred_element_type=jnp.float32)
        for t in range(9):
            parts[9 * i + t] = terms[:, t * LANES:(t + 1) * LANES]
        while done < groups and min(taps, (done + 1) * group) <= 9 * (i + 1):
            sources = [parts[t] for t in range(done * group, min(taps, (done + 1) * group))]
            for lt in range(per_group):
                tile = rearrange(sources, outputs, lt * LANES, LANES)
                for rt in range(row_tiles):
                    gwf[place(state["stored"])] = tile[rt * SUB:(rt + 1) * SUB]
                    state["stored"] += 1
            done += 1
        if i == 2:
            while state["stored"] < U * unit_tiles:
                gwf[place(state["stored"])] = jnp.zeros((SUB, LANES), jnp.float32)
                state["stored"] += 1
        send_ready()

    def conv(i):
        weights = wide[:, 9 * LANES * i:9 * LANES * (i + 1)]
        return lax.dot_general(window(i), weights, NT, preferred_element_type=jnp.float32)

    def after_a(u):
        for d in order:
            value = gwf[u, pair, chunk(d)]
            if PR == 2:
                stage_a(u, d).wait_recv()
                value = value + recv_a[u, d - 1]
            sum_a[u, d - 1] = value
            send_b[u, d - 1] = value.astype(jnp.bfloat16)
            for e in range(1, X):
                stage_b(u, d, e).start()

    def after_b(u):
        for d in order:
            value = sum_a[u, d - 1, x]
            for e in range(1, X):
                stage_b(u, d, e).wait_recv()
                value = value + recv_b[u, d - 1, e - 1].astype(jnp.float32)
            if d < R:
                send_c[u, d - 1] = value.astype(jnp.bfloat16)
                stage_c(u, d).start()
            else:
                sum_b[u] = value

    def after_c(u):
        value = sum_b[u]
        for d in range(1, R):
            stage_c(u, d).wait_recv()
            value = value + recv_c[u, d - 1].astype(jnp.float32)
        gath[u, pair, z, x] = value.astype(jnp.bfloat16)
        for d in range(1, R):
            gather_c(u, d).start()
        for e in range(1, X):
            gather_b(u, R, e).start()

    def after_gather_c(u):
        for d in range(1, R):
            gather_c(u, d).wait_recv()
            for e in range(1, X):
                gather_b(u, d, e).start()

    def after_gather_b(u):
        for d in mine_first:
            for e in range(1, X):
                gather_b(u, d, e).wait_recv()
            if PR == 2:
                gather_a(u, d).start()

    def after_gather_a(u):
        if PR == 2:
            for d in mine_first:
                gather_a(u, d).wait_recv()

    def unpack(g):
        first = g * per_group * row_tiles
        sources = [
            jnp.concatenate(
                [gath[place(first + lt * row_tiles + rt)] for rt in range(row_tiles)], axis=0
            ).astype(jnp.float32)
            for lt in range(per_group)
        ]
        for a in range(min(group, taps - g * group)):
            value = rearrange(sources, LANES, a * outputs, outputs)
            out_ref[g * group + a] = value[:, :outputs].astype(jnp.bfloat16)

    def finish_features(first, last):
        for f in range(first, last):
            inv_rms, unit, normed, sigma = activate(f)
            grad_act = acc[f * height * width:(f + 1) * height * width]
            grad_normed = grad_act * sigma * (1.0 + normed * (1.0 - sigma))
            grad_unit = grad_normed * gain[...]
            along = jnp.sum(grad_unit * unit, axis=-1, keepdims=True) / channels
            result = inv_rms * (grad_unit - unit * along)
            gf_ref[f] = result.astype(jnp.bfloat16).reshape(height, width, channels)

    after_a(0)
    loads[3].wait()
    wide[...] = jnp.zeros(wide.shape, wide.dtype)
    for t in range(taps):
        wide[:, t * LANES:t * LANES + outputs] = weight[t]
    for u in range(1, U):
        after_a(u)
    acc[...] = conv(0)
    after_b(0)
    acc[...] += conv(1)
    for u in range(1, U):
        after_b(u)
    after_c(0)
    acc[...] += conv(2)
    for u in range(1, U):
        after_c(u)
    after_gather_c(0)
    half = frames // 2
    finish_features(0, half)
    for u in range(1, U):
        after_gather_c(u)
    after_gather_b(0)
    finish_features(half, frames)
    for u in range(1, U):
        after_gather_b(u)
    unpacked = 0
    for u in range(U):
        after_gather_a(u)
        while unpacked < groups and (unpacked + 1) * per_group * row_tiles <= (u + 1) * unit_tiles:
            unpack(unpacked)
            unpacked += 1

    for n in range(5):
        @pl.when(halos[n][0])
        def _():
            halo(n).wait_send()
    for u in range(U):
        for d in order:
            if PR == 2:
                stage_a(u, d).wait_send()
                gather_a(u, d).wait_send()
            for e in range(1, X):
                stage_b(u, d, e).wait_send()
                gather_b(u, d, e).wait_send()
            if d < R:
                stage_c(u, d).wait_send()
                gather_c(u, d).wait_send()


def on_device(features, norm_gain, conv_weight, out_grad):
    frames, height, width, channels = features.shape
    outputs = out_grad.shape[3]
    T, R = lax.axis_size("tm"), lax.axis_size("rows")
    PR = 2 if T % 2 == 0 else 1
    X = T // PR
    U = 2
    kernels = conv_weight.shape[:3]
    taps = math.prod(kernels)
    group = LANES // math.gcd(LANES, outputs)
    per_group = group * outputs // LANES
    row_tiles = channels // SUB
    groups = -(-taps // group)
    m = -(-(groups * per_group * row_tiles) // (U * T * R))
    count = frames * height * width
    bf16, f32 = jnp.bfloat16, jnp.float32
    vmem, dma = pltpu.VMEM, pltpu.SemaphoreType.DMA
    tile = (m, SUB, LANES)
    rest = max(R - 1, 1)
    sides = max(X - 1, 1)
    in_vmem = pl.BlockSpec(memory_space=pltpu.VMEM)
    in_hbm = pl.BlockSpec(memory_space=pltpu.HBM)
    grad_features, kernel_sum = pl.pallas_call(
        functools.partial(kernel, (T, R, PR, X, U, m)),
        out_shape=(
            jax.ShapeDtypeStruct(features.shape, bf16),
            jax.ShapeDtypeStruct((taps, channels, outputs), bf16),
        ),
        in_specs=[in_hbm] * 4,
        out_specs=(in_vmem, in_vmem),
        scratch_shapes=[
            vmem(features.shape, bf16),
            vmem((1, channels), f32),
            vmem((taps, channels, outputs), bf16),
            vmem((frames + 2, height + 2, width, outputs), bf16),
            vmem((frames + 2, height + 2, width, 3 * LANES), bf16),
            vmem((channels, taps * LANES), bf16),
            vmem((channels, count), bf16),
            vmem((count, channels), f32),
            vmem((taps, channels, LANES), f32),
            vmem((U, PR, R, X) + tile, f32),
            vmem((U, R, X) + tile, f32),
            vmem((U, R, X) + tile, f32),
            vmem((U, R, X) + tile, bf16),
            vmem((U, R, sides) + tile, bf16),
            vmem((U,) + tile, f32),
            vmem((U, rest) + tile, bf16),
            vmem((U, rest) + tile, bf16),
            vmem((U, PR, R, X) + tile, bf16),
            dma((4,)),
            dma((5,)), dma((5,)),
            dma((U, R)), dma((U, R)),
            dma((U, R, sides)), dma((U, R, sides)),
            dma((U, rest)), dma((U, rest)),
            dma((U, rest)), dma((U, rest)),
            dma((U, R, sides)), dma((U, R, sides)),
            dma((U, R)), dma((U, R)),
        ],
        compiler_params=pltpu.CompilerParams(
            collective_id=0, has_side_effects=True, vmem_limit_bytes=50 * 1024 * 1024
        ),
    )(
        *(
            pltpu.with_memory_space_constraint(array, pltpu.HBM)
            for array in (
                features, norm_gain.reshape(1, channels),
                conv_weight.reshape(taps, channels, outputs), out_grad,
            )
        )
    )
    scale = 1.0 / math.sqrt(count * T * R)
    grad_weight = kernel_sum.astype(f32) * scale
    return grad_features, grad_weight.reshape(kernels + (channels, outputs))


def solution(mesh):
    split = P(("clips", "tm"), "rows", None, None)
    return jax.shard_map(
        on_device,
        mesh=mesh,
        in_specs=(split, P(), P(), split),
        out_specs=(split, P("clips", None, None, None, None)),
        check_vma=False,
    )
```

```python
import functools
import math

import jax
import jax.numpy as jnp
from jax import lax
from jax.experimental import pallas as pl
from jax.experimental.pallas import tpu as pltpu
from jax.sharding import PartitionSpec as P

LANES = 128
SUB = 16
MESH = pl.DeviceIdType.MESH
NT = (((1,), (1,)), ((), ()))


def shift_lanes(x, shift):
    shift = shift % LANES
    return x if shift == 0 else pltpu.roll(x, shift, 1)


def rearrange(sources, source_width, target_start, target_width):
    lane = lax.broadcasted_iota(jnp.int32, (1, LANES), 1)
    value = None
    for a, source in enumerate(sources):
        first = a * source_width - target_start
        if first >= target_width or first + source_width <= 0:
            continue
        moved = shift_lanes(source, first)
        value = moved if value is None else jnp.where(lane >= first, moved, value)
    return value


def kernel(
    dims,
    features_hbm, gain_hbm, weight_hbm, grad,
    gf_ref, out_ref,
    features, gain, weight, padded, shifted, wide, act_t, acc, parts, gwf, recv_a, sum_a,
    send_b, recv_b, sum_b, send_c, recv_c, gath,
    local, halo_s, halo_r, sa, ra, sb, rb, sc, rc, sc2, rc2, sb2, rb2, sa2, ra2,
):
    T, R, PR, X, U, m = dims
    frames, height, width, channels = features.shape
    outputs = grad.shape[3]
    taps = weight.shape[0]
    tm, z = lax.axis_index("tm"), lax.axis_index("rows")
    pair, x = lax.rem(tm, PR), lax.div(tm, PR)
    own = pl.ds(1, height)
    tail = pl.ds(frames, 2)
    body = pl.ds(0, frames)

    loads = [
        pltpu.make_async_copy(source, target, local.at[n])
        for n, (source, target) in enumerate((
            (features_hbm, features), (gain_hbm, gain),
            (grad, padded.at[body, own]), (weight_hbm, weight),
        ))
    ]
    for load in loads:
        load.start()

    barrier = pltpu.get_barrier_semaphore()
    for d in range(1, T * R):
        peer = lax.rem(tm * R + z + d, T * R)
        pl.semaphore_signal(
            barrier, inc=1, device_id={"tm": lax.div(peer, R), "rows": lax.rem(peer, R)},
            device_id_type=MESH,
        )

    up, down, later, earlier = z > 0, z < R - 1, tm < T - 1, tm > 0
    halos = (
        (down, (tm, z + 1), up, grad.at[:, height - 1], padded.at[body, 0]),
        (up, (tm, z - 1), down, grad.at[:, 0], padded.at[body, height + 1]),
        (earlier, (tm - 1, z), later, grad.at[pl.ds(0, 2)], padded.at[tail, own]),
        (jnp.logical_and(earlier, down), (tm - 1, z + 1), jnp.logical_and(later, up),
         grad.at[pl.ds(0, 2), height - 1], padded.at[tail, 0]),
        (jnp.logical_and(earlier, up), (tm - 1, z - 1), jnp.logical_and(later, down),
         grad.at[pl.ds(0, 2), 0], padded.at[tail, height + 1]),
    )

    def halo(n):
        _, to, _, source, target = halos[n]
        return pltpu.make_async_remote_copy(
            src_ref=source, dst_ref=target, send_sem=halo_s.at[n], recv_sem=halo_r.at[n],
            device_id={"tm": to[0], "rows": to[1]}, device_id_type=MESH,
        )

    for n, (_, _, receives, _, target) in enumerate(halos):
        @pl.when(jnp.logical_not(receives))
        def _():
            target[...] = jnp.zeros(target.shape, target.dtype)
    shifted[:, :, :, LANES:2 * LANES] = jnp.zeros(shifted.shape[:3] + (LANES,), shifted.dtype)

    pl.semaphore_wait(barrier, T * R - 1)
    for n in range(5):
        @pl.when(halos[n][0])
        def _():
            halo(n).start()

    def activate(f):
        values = features[f].reshape(height * width, channels).astype(jnp.float32)
        inv_rms = lax.rsqrt(jnp.sum(values * values, axis=-1, keepdims=True) / channels + 1e-06)
        unit = values * inv_rms
        normed = unit * gain[...]
        sigma = 1.0 / (1.0 + jnp.exp(-normed))
        return inv_rms, unit, normed, sigma

    loads[0].wait()
    loads[1].wait()
    for f in range(frames):
        _, _, normed, sigma = activate(f)
        act = (normed * sigma).astype(jnp.bfloat16)
        act_t[:, f * height * width:(f + 1) * height * width] = act.T

    loads[2].wait()
    for n in range(5):
        @pl.when(halos[n][2])
        def _():
            halo(n).wait_recv()

    rows = (height + 2) * width
    column = lax.rem(lax.broadcasted_iota(jnp.int32, (rows, LANES), 0), width)
    for f in range(frames + 2):
        shifted[f, :, :, LANES:LANES + outputs] = padded[f]
        middle = shifted[f, :, :, LANES:2 * LANES].reshape(rows, LANES).astype(jnp.float32)
        after = jnp.where(column == width - 1, 0.0, pltpu.roll(middle, rows - 1, 0))
        before = jnp.where(column == 0, 0.0, pltpu.roll(middle, 1, 0))
        shape = (height + 2, width, LANES)
        shifted[f, :, :, 0:LANES] = after.astype(jnp.bfloat16).reshape(shape)
        shifted[f, :, :, 2 * LANES:3 * LANES] = before.astype(jnp.bfloat16).reshape(shape)

    count = frames * height * width

    def window(i):
        return jnp.concatenate(
            [
                shifted[2 - i:2 - i + frames, 2 - j:2 - j + height].reshape(count, 3 * LANES)
                for j in range(3)
            ],
            axis=1,
        )

    def remote(source, target, send, recv, to_tm, to_z):
        return pltpu.make_async_remote_copy(
            src_ref=source, dst_ref=target, send_sem=send, recv_sem=recv,
            device_id={"tm": to_tm, "rows": to_z}, device_id_type=MESH,
        )

    mate = x * PR + (1 - pair if PR == 2 else pair)

    def chunk(d):
        return lax.rem(z + d, R)

    def back(d):
        return lax.rem(z + 2 * R - d, R)

    def side(e):
        return lax.rem(x + e, X)

    def stage_a(u, d):
        return remote(
            gwf.at[u, 1 - pair, chunk(d)], recv_a.at[u, d - 1],
            sa.at[u, d - 1], ra.at[u, d - 1], mate, z,
        )

    def stage_b(u, d, e):
        return remote(
            send_b.at[u, d - 1, side(e)], recv_b.at[u, d - 1, e - 1],
            sb.at[u, d - 1, e - 1], rb.at[u, d - 1, e - 1], side(e) * PR + pair, z,
        )

    def stage_c(u, d):
        return remote(
            send_c.at[u, d - 1], recv_c.at[u, d - 1],
            sc.at[u, d - 1], rc.at[u, d - 1], tm, chunk(d),
        )

    def gather_c(u, d):
        piece = gath.at[u, pair, z, x]
        return remote(piece, piece, sc2.at[u, d - 1], rc2.at[u, d - 1], tm, chunk(d))

    def gather_b(u, d, e):
        piece = gath.at[u, pair, back(d), x]
        return remote(
            piece, piece, sb2.at[u, d - 1, e - 1], rb2.at[u, d - 1, e - 1],
            side(e) * PR + pair, z,
        )

    def gather_a(u, d):
        piece = gath.at[u, pair, back(d)]
        return remote(piece, piece, sa2.at[u, d - 1], ra2.at[u, d - 1], mate, z)

    order = range(1, R + 1)
    low = 1 - lax.div(2 * z, R)
    nearest = [low * (R - d) + (1 - low) * d for d in range(1, R)]
    mine_first = (R, *nearest)
    group = LANES // math.gcd(LANES, outputs)
    groups = -(-taps // group)
    per_group = group * outputs // LANES
    row_tiles = channels // SUB
    unit_tiles = T * R * m

    def place(n):
        n, s = divmod(n, m)
        n, xx = divmod(n, X)
        n, c = divmod(n, R)
        u, pp = divmod(n, PR)
        return u, pp, c, xx, s

    state = {"stored": 0, "sent": 0}

    def send_ready():
        while (state["sent"] + 1) * unit_tiles <= state["stored"]:
            if PR == 2:
                for d in order:
                    stage_a(state["sent"], d).start()
            state["sent"] += 1

    done = 0
    for i in range(3):
        terms = jnp.dot(act_t[...], window(i), preferred_element_type=jnp.float32)
        for t in range(9):
            parts[9 * i + t] = terms[:, t * LANES:(t + 1) * LANES]
        while done < groups and min(taps, (done + 1) * group) <= 9 * (i + 1):
            sources = [parts[t] for t in range(done * group, min(taps, (done + 1) * group))]
            for lt in range(per_group):
                tile = rearrange(sources, outputs, lt * LANES, LANES)
                for rt in range(row_tiles):
                    gwf[place(state["stored"])] = tile[rt * SUB:(rt + 1) * SUB]
                    state["stored"] += 1
            done += 1
        if i == 2:
            while state["stored"] < U * unit_tiles:
                gwf[place(state["stored"])] = jnp.zeros((SUB, LANES), jnp.float32)
                state["stored"] += 1
        send_ready()

    def conv(i):
        weights = wide[:, 9 * LANES * i:9 * LANES * (i + 1)]
        return lax.dot_general(window(i), weights, NT, preferred_element_type=jnp.float32)

    def after_a(u):
        for d in order:
            value = gwf[u, pair, chunk(d)]
            if PR == 2:
                stage_a(u, d).wait_recv()
                value = value + recv_a[u, d - 1]
            sum_a[u, d - 1] = value
            send_b[u, d - 1] = value.astype(jnp.bfloat16)
            for e in range(1, X):
                stage_b(u, d, e).start()

    def after_b(u):
        for d in order:
            value = sum_a[u, d - 1, x]
            for e in range(1, X):
                stage_b(u, d, e).wait_recv()
                value = value + recv_b[u, d - 1, e - 1].astype(jnp.float32)
            if d < R:
                send_c[u, d - 1] = value.astype(jnp.bfloat16)
                stage_c(u, d).start()
            else:
                sum_b[u] = value

    def after_c(u):
        value = sum_b[u]
        for d in range(1, R):
            stage_c(u, d).wait_recv()
            value = value + recv_c[u, d - 1].astype(jnp.float32)
        gath[u, pair, z, x] = value.astype(jnp.bfloat16)
        for d in range(1, R):
            gather_c(u, d).start()
        for e in range(1, X):
            gather_b(u, R, e).start()

    def after_gather_c(u):
        for d in nearest:
            gather_c(u, d).wait_recv()
            for e in range(1, X):
                gather_b(u, d, e).start()

    def after_gather_b(u):
        for d in mine_first:
            for e in range(1, X):
                gather_b(u, d, e).wait_recv()
            if PR == 2:
                gather_a(u, d).start()

    def after_gather_a(u):
        if PR == 2:
            for d in mine_first:
                gather_a(u, d).wait_recv()

    def unpack(g):
        first = g * per_group * row_tiles
        sources = [
            jnp.concatenate(
                [gath[place(first + lt * row_tiles + rt)] for rt in range(row_tiles)], axis=0
            ).astype(jnp.float32)
            for lt in range(per_group)
        ]
        for a in range(min(group, taps - g * group)):
            value = rearrange(sources, LANES, a * outputs, outputs)
            out_ref[g * group + a] = value[:, :outputs].astype(jnp.bfloat16)

    def finish_features(first, last):
        for f in range(first, last):
            inv_rms, unit, normed, sigma = activate(f)
            grad_act = acc[f * height * width:(f + 1) * height * width]
            grad_normed = grad_act * sigma * (1.0 + normed * (1.0 - sigma))
            grad_unit = grad_normed * gain[...]
            along = jnp.sum(grad_unit * unit, axis=-1, keepdims=True) / channels
            result = inv_rms * (grad_unit - unit * along)
            gf_ref[f] = result.astype(jnp.bfloat16).reshape(height, width, channels)

    after_a(0)
    loads[3].wait()
    wide[...] = jnp.zeros(wide.shape, wide.dtype)
    for t in range(taps):
        wide[:, t * LANES:t * LANES + outputs] = weight[t]
    for u in range(1, U):
        after_a(u)
    acc[...] = conv(0)
    after_b(0)
    acc[...] += conv(1)
    for u in range(1, U):
        after_b(u)
    after_c(0)
    acc[...] += conv(2)
    for u in range(1, U):
        after_c(u)
    after_gather_c(0)
    half = frames // 2
    finish_features(0, half)
    for u in range(1, U):
        after_gather_c(u)
    after_gather_b(0)
    finish_features(half, frames)
    for u in range(1, U):
        after_gather_b(u)
    unpacked = 0
    for u in range(U):
        after_gather_a(u)
        while unpacked < groups and (unpacked + 1) * per_group * row_tiles <= (u + 1) * unit_tiles:
            unpack(unpacked)
            unpacked += 1

    for n in range(5):
        @pl.when(halos[n][0])
        def _():
            halo(n).wait_send()
    for u in range(U):
        for d in order:
            if PR == 2:
                stage_a(u, d).wait_send()
                gather_a(u, d).wait_send()
            for e in range(1, X):
                stage_b(u, d, e).wait_send()
                gather_b(u, d, e).wait_send()
            if d < R:
                stage_c(u, d).wait_send()
                gather_c(u, d).wait_send()


def on_device(features, norm_gain, conv_weight, out_grad):
    frames, height, width, channels = features.shape
    outputs = out_grad.shape[3]
    T, R = lax.axis_size("tm"), lax.axis_size("rows")
    PR = 2 if T % 2 == 0 else 1
    X = T // PR
    U = 2
    kernels = conv_weight.shape[:3]
    taps = math.prod(kernels)
    group = LANES // math.gcd(LANES, outputs)
    per_group = group * outputs // LANES
    row_tiles = channels // SUB
    groups = -(-taps // group)
    m = -(-(groups * per_group * row_tiles) // (U * T * R))
    count = frames * height * width
    bf16, f32 = jnp.bfloat16, jnp.float32
    vmem, dma = pltpu.VMEM, pltpu.SemaphoreType.DMA
    tile = (m, SUB, LANES)
    rest = max(R - 1, 1)
    sides = max(X - 1, 1)
    in_vmem = pl.BlockSpec(memory_space=pltpu.VMEM)
    in_hbm = pl.BlockSpec(memory_space=pltpu.HBM)
    grad_features, kernel_sum = pl.pallas_call(
        functools.partial(kernel, (T, R, PR, X, U, m)),
        out_shape=(
            jax.ShapeDtypeStruct(features.shape, bf16),
            jax.ShapeDtypeStruct((taps, channels, outputs), bf16),
        ),
        in_specs=[in_hbm] * 4,
        out_specs=(in_vmem, in_vmem),
        scratch_shapes=[
            vmem(features.shape, bf16),
            vmem((1, channels), f32),
            vmem((taps, channels, outputs), bf16),
            vmem((frames + 2, height + 2, width, outputs), bf16),
            vmem((frames + 2, height + 2, width, 3 * LANES), bf16),
            vmem((channels, taps * LANES), bf16),
            vmem((channels, count), bf16),
            vmem((count, channels), f32),
            vmem((taps, channels, LANES), f32),
            vmem((U, PR, R, X) + tile, f32),
            vmem((U, R, X) + tile, f32),
            vmem((U, R, X) + tile, f32),
            vmem((U, R, X) + tile, bf16),
            vmem((U, R, sides) + tile, bf16),
            vmem((U,) + tile, f32),
            vmem((U, rest) + tile, bf16),
            vmem((U, rest) + tile, bf16),
            vmem((U, PR, R, X) + tile, bf16),
            dma((4,)),
            dma((5,)), dma((5,)),
            dma((U, R)), dma((U, R)),
            dma((U, R, sides)), dma((U, R, sides)),
            dma((U, rest)), dma((U, rest)),
            dma((U, rest)), dma((U, rest)),
            dma((U, R, sides)), dma((U, R, sides)),
            dma((U, R)), dma((U, R)),
        ],
        compiler_params=pltpu.CompilerParams(
            collective_id=0, has_side_effects=True, vmem_limit_bytes=50 * 1024 * 1024
        ),
    )(
        *(
            pltpu.with_memory_space_constraint(array, pltpu.HBM)
            for array in (
                features, norm_gain.reshape(1, channels),
                conv_weight.reshape(taps, channels, outputs), out_grad,
            )
        )
    )
    scale = 1.0 / math.sqrt(count * T * R)
    grad_weight = kernel_sum.astype(f32) * scale
    return grad_features, grad_weight.reshape(kernels + (channels, outputs))


def solution(mesh):
    split = P(("clips", "tm"), "rows", None, None)
    return jax.shard_map(
        on_device,
        mesh=mesh,
        in_specs=(split, P(), P(), split),
        out_specs=(split, P("clips", None, None, None, None)),
        check_vma=False,
    )
```
